32 devices in a mesh: clip: 2 (over y), tile: 4 (over z), slab: 2 (over x), chan: 2 (over core).
Axes of the slice: x: 2, y: 2, z: 4, core: 2. Of those that a mesh axis runs over, the one named last changes fastest.
Arguments:
- video: bfloat16 [16, 16, 128, 128], P(('clip', 'slab'), 'tile'), parts along dimension 0, may hold values from -6 to 6
- first_weight: bfloat16 [3, 3, 3, 128, 128], P(None, None, None, None, 'chan'), may hold values from -0.109375 to 0.109375
- first_bias: float32 [128], P('chan'), may hold values from -3 to 3
- second_weight: bfloat16 [3, 3, 3, 128, 256], replicated, may hold values from -0.109375 to 0.109375
- second_bias: float32 [256], P('chan'), may hold values from -3 to 3
Outputs:
- latents: bfloat16 [8, 16, 128, 256], P(('clip', 'slab'), 'tile', None, 'chan'), parts along dimension 0
The draws below stay inside these ranges and needn't reach their ends.
There are 2 independent parts, one for each index of `clip`. The reference program is written for one: setup_inputs(seed, part) draws one part's arguments, and reference() takes and returns one part's arrays. A program takes and returns all parts, laid end to end along the dimension named above; an argument that names none is the same for every part. Nothing has to cross between parts.
All inputs are finite; a program needn't handle non-finite values.
Results may differ from the reference program's by a relative error of at most 0.0095.
Values may be sent and summed in bfloat16 or wider, within the bound.
A program may use at most 64 MiB of HBM per device.

```python
import jax
import jax.numpy as jnp
from jax import lax

CH_IN = 128
CH_MID = 128
CH_OUT = 256
W = 128
FRAMES = 8
HEIGHT = 16


def level_of(stream_key, shape, cuts, smallest, largest):
    def one(dim, parts):
        heights = jax.random.uniform(jax.random.fold_in(jax.random.fold_in(stream_key, 6), dim), (parts,), jnp.float32, smallest / len(cuts), largest / len(cuts))
        return jnp.repeat(jnp.exp(heights), shape[dim] // parts).reshape((-1,) + (1,) * (len(shape) - dim - 1))

    level = one(*cuts[0])
    for cut in cuts[1:]:
        level = level * one(*cut)
    return level


def scatter_about(rng, shape, spread, limit, shards=(), dtype=jnp.bfloat16):
    factor_of = level_of(rng, shape, shards, -0.22, 0.18) if shards else 1.0
    entries = jax.random.normal(rng, shape, jnp.float32) * spread * factor_of
    return jnp.minimum(jnp.maximum(entries, -limit), limit).astype(dtype)


def setup_inputs(seed: int = 0, part: int = 0) -> dict:
    arg_keys = jax.random.split(jax.random.key(seed), 6)
    part_keys = jax.random.split(jax.random.fold_in(arg_keys[5], part), 6)
    video = scatter_about(part_keys[0], (FRAMES, HEIGHT, W, CH_IN), 1.0, 6.0, ((0, 2), (1, 4)))
    first_weight = scatter_about(arg_keys[1], (3, 3, 3, CH_IN, CH_MID), (27 * CH_IN) ** -0.5, 0.109375, ((4, 2),))
    first_bias = scatter_about(arg_keys[2], (CH_MID,), 0.5, 3.0, ((0, 2),), jnp.float32)
    second_weight = scatter_about(arg_keys[3], (3, 3, 3, CH_MID, CH_OUT), (27 * CH_MID) ** -0.5, 0.109375)
    second_bias = scatter_about(arg_keys[4], (CH_OUT,), 0.5, 3.0, ((0, 2),), jnp.float32)
    return {"video": video, "first_weight": first_weight, "first_bias": first_bias, "second_weight": second_weight, "second_bias": second_bias}


def causal_convolve(source, kernel, stride):
    result = lax.conv_general_dilated(source[None], kernel, window_strides=(stride, 1, 1), padding=((2, 0), (1, 1), (1, 1)), dimension_numbers=("NDHWC", "DHWIO", "NDHWC"), preferred_element_type=jnp.float32)
    return result[0]


def reference(video, first_weight, first_bias, second_weight, second_bias):
    hidden = jax.nn.silu(causal_convolve(video, first_weight, 1) + first_bias).astype(jnp.bfloat16)
    return jax.nn.silu(causal_convolve(hidden, second_weight, 2) + second_bias).astype(jnp.bfloat16)
```

```python
import functools

import jax
import jax.numpy as jnp
from jax import lax
from jax.experimental import pallas as pl
from jax.experimental.pallas import tpu as pltpu
from jax.sharding import PartitionSpec as P

MESH = pl.DeviceIdType.MESH
BACK = 4


def kernel(
    tiles, slabs, video, w1, b1, w2, b2, out,
    v, h, k1, k2, b1_peer, b2_peer, going,
    local_sem, w1_sem, w2_sem, small_send, small_recv, own_send, own_recv,
    x_send, x_recv, z_send, z_recv, p_send, p_recv, o_send, o_recv,
):
    frames, rows, columns, channels = video.shape
    half = rows // 2
    core = lax.axis_index("chan")
    tile = lax.axis_index("tile")
    slab = lax.axis_index("slab")
    other = 1 - core
    z_tile = tile + 2 * core - 1
    has_z = jnp.logical_and(z_tile >= 0, z_tile < tiles)
    no_z = jnp.logical_or(z_tile < 0, z_tile >= tiles)
    has_next = slab < slabs - 1
    has_prev = slab > 0
    peer = {"chan": other}
    z_peer = {"chan": other, "tile": z_tile}
    following = {"slab": slab + 1}
    preceding = {"slab": slab - 1}

    def remote(src, dst, send, recv, device):
        return pltpu.make_async_remote_copy(
            src_ref=src, dst_ref=dst, send_sem=send, recv_sem=recv,
            device_id=device, device_id_type=MESH,
        )

    mine = pl.ds(half * core, half)
    halo_here = pl.ds(rows * core, half)
    halo_there = pl.ds(rows * other, half)
    inner_here = pl.ds(rows * other, half)
    inner_there = pl.ds(rows * core, half)
    arrived = pl.ds(half, half)

    into_v = pltpu.make_async_copy(
        video.at[pl.ds(0, frames - 1)],
        v.at[pl.ds(BACK, frames - 1), pl.ds(half * other, rows)],
        local_sem,
    )
    into_v.start()
    own_w1 = pltpu.make_async_copy(w1, k1.at[:, :, 0], w1_sem)
    own_w1.start()
    part = channels // 2
    width = b2.shape[1]
    w2_copies = []
    for e in range(3):
        for n in range(2):
            for k in range(2):
                owner_n = core if n == 0 else other
                owner_k = core if k == 0 else other
                w2_copies.append(
                    pltpu.make_async_copy(
                        w2.at[:, e, pl.ds(pl.multiple_of(owner_k * part, part), part),
                              pl.ds(pl.multiple_of(owner_n * width, width), width)],
                        k2.at[:, pl.ds(k * part, part), pl.ds((2 * e + n) * width, width)],
                        w2_sem.at[len(w2_copies)],
                    )
                )
    for copy in w2_copies:
        copy.start()

    barrier = pltpu.get_barrier_semaphore()
    everyone = ((None, peer), (has_z, z_peer), (has_next, following), (has_prev, preceding))

    def when(condition, body):
        if condition is None:
            body()
        else:
            pl.when(condition)(body)

    for condition, device in everyone:
        when(condition, lambda device=device: pl.semaphore_signal(
            barrier, inc=1, device_id=device, device_id_type=MESH))
    met = 1 + sum(jnp.where(condition, 1, 0) for condition, _ in everyone[1:])
    pl.semaphore_wait(barrier, met)

    small = [
        remote(w1, k1.at[:, :, 1], small_send.at[0], small_recv.at[0], peer),
        remote(b1, b1_peer, small_send.at[1], small_recv.at[1], peer),
        remote(b2, b2_peer, small_send.at[2], small_recv.at[2], peer),
    ]
    to_next = [
        remote(video.at[frames - BACK + f, mine], v.at[f, arrived], x_send.at[f], x_recv.at[f], following)
        for f in range(BACK)
    ]
    own_z = remote(
        video.at[pl.ds(0, frames - 1), mine],
        v.at[pl.ds(BACK, frames - 1), halo_there],
        own_send, own_recv, z_peer,
    )
    forward_z = [
        remote(v.at[f, arrived], v.at[f, halo_there], z_send.at[f], z_recv.at[f], z_peer)
        for f in range(BACK)
    ]
    forward_p = [
        remote(v.at[f, arrived], v.at[f, inner_there], p_send.at[f], p_recv.at[f], peer)
        for f in range(BACK)
    ]

    small[0].start()

    @pl.when(has_next)
    def _():
        for f in reversed(range(BACK)):
            to_next[f].start()

    @pl.when(has_z)
    def _():
        own_z.start()

    small[1].start()
    small[2].start()

    @pl.when(no_z)
    def _():
        v[:, halo_here] = jnp.zeros((v.shape[0], half, columns, channels), v.dtype)

    @pl.when(slab == 0)
    def _():
        v[0:BACK] = jnp.zeros((BACK,) + v.shape[1:], v.dtype)
        h[0:2] = jnp.zeros((2,) + h.shape[1:], h.dtype)

    def pass_on(f):
        @pl.when(has_prev)
        def _():
            remote(v.at[f, arrived], v.at[f, arrived], x_send.at[f], x_recv.at[f], preceding).wait_recv()
            forward_p[f].start()

            @pl.when(has_z)
            def _():
                forward_z[f].start()

    def ready(f):
        @pl.when(has_prev)
        def _():
            remote(v.at[f, arrived], v.at[f, inner_here], p_send.at[f], p_recv.at[f], peer).wait_recv()

            @pl.when(has_z)
            def _():
                remote(v.at[f, arrived], v.at[f, halo_here], z_send.at[f], z_recv.at[f], z_peer).wait_recv()

    def taps(source, first, count):
        return jnp.concatenate(
            [
                source[first + a, b : b + count].reshape(count * columns, channels)
                for a in range(3)
                for b in range(3)
            ],
            axis=1,
        )

    def shifted_sum(parts, width, bias):
        size = parts.shape[0]
        column = lax.broadcasted_iota(jnp.int32, (size, width), 0) % columns
        before = pltpu.roll(parts[:, 0:width], 1, 0)
        after = pltpu.roll(parts[:, 2 * width : 3 * width], size - 1, 0)
        total = parts[:, width : 2 * width] + jnp.where(column == 0, 0.0, before)
        total = total + jnp.where(column == columns - 1, 0.0, after) + bias
        return total / (1.0 + jnp.exp(-total))

    def hidden(index):
        count = h.shape[1]
        parts = lax.dot_general(
            taps(v, index, count),
            jnp.concatenate([k1[tap].reshape(3 * channels, channels) for tap in range(9)], axis=1),
            (((1,), (1,)), ((), ())),
            preferred_element_type=jnp.float32,
        )
        bias = jnp.concatenate([b1[...], b1_peer[...]], axis=1)
        value = shifted_sum(parts, channels, bias).astype(h.dtype)
        h[index] = value.reshape(count, columns, channels)

        @pl.when(no_z)
        def _():
            h[index, pl.ds((count - 1) * core, 1)] = jnp.zeros((1, columns, channels), h.dtype)

    to_peer = [
        remote(going.at[t], out.at[t, mine], o_send.at[t], o_recv.at[t], peer)
        for t in range(frames // 2)
    ]

    def latent(t):
        parts = jnp.dot(
            taps(h, 2 * t, half), k2[...].reshape(9 * channels, 6 * width),
            preferred_element_type=jnp.float32,
        )
        bias = jnp.concatenate([b2[...], b2_peer[...]], axis=1)
        value = shifted_sum(parts, 2 * width, bias).astype(out.dtype)
        going[t] = value[:, width:].reshape(half, columns, width)
        to_peer[t].start()
        out[t, mine] = value[:, :width].reshape(half, columns, width)

    small[0].wait_recv()
    own_w1.wait()
    small[1].wait_recv()
    small[2].wait_recv()
    pass_on(BACK - 1)
    into_v.wait()

    @pl.when(has_z)
    def _():
        remote(
            v.at[pl.ds(BACK, frames - 1), halo_here], v.at[pl.ds(BACK, frames - 1), halo_here],
            own_send, own_recv, z_peer,
        ).wait_recv()

    for index in range(BACK, frames + 1):
        hidden(index)
    pass_on(2)
    ready(3)
    hidden(3)
    pass_on(1)
    pass_on(0)
    ready(2)
    hidden(2)
    for copy in w2_copies:
        copy.wait()
    for t in range(1, frames // 2):
        latent(t)
    ready(1)

    @pl.when(has_prev)
    def _():
        hidden(1)

    ready(0)

    @pl.when(has_prev)
    def _():
        hidden(0)

    latent(0)

    for copy in small:
        copy.wait_send()

    @pl.when(has_next)
    def _():
        for copy in to_next:
            copy.wait_send()

    @pl.when(has_z)
    def _():
        own_z.wait_send()

    @pl.when(has_prev)
    def _():
        for copy in forward_p:
            copy.wait_send()

        @pl.when(has_z)
        def _():
            for copy in forward_z:
                copy.wait_send()

    theirs = pl.ds(half * other, half)
    for t in range(frames // 2):
        remote(going.at[t], out.at[t, theirs], o_send.at[t], o_recv.at[t], peer).wait_recv()
        to_peer[t].wait_send()


def shards(tiles, slabs, video, first_weight, first_bias, second_weight, second_bias):
    frames, rows, columns, channels = video.shape
    half = rows // 2
    assert half == 2 and frames >= BACK and frames % 2 == 0
    part = first_bias.shape[0]
    width = second_bias.shape[0]
    anywhere = pl.BlockSpec(memory_space=pl.ANY)
    inside = pl.BlockSpec(memory_space=pltpu.VMEM)
    dma = pltpu.SemaphoreType.DMA
    return pl.pallas_call(
        functools.partial(kernel, tiles, slabs),
        out_shape=jax.ShapeDtypeStruct((frames // 2, rows, columns, width), jnp.bfloat16),
        in_specs=[anywhere, anywhere, inside, anywhere, inside],
        out_specs=inside,
        scratch_shapes=[
            pltpu.VMEM((BACK + frames - 1, rows + 2, columns, channels), jnp.bfloat16),
            pltpu.VMEM((frames + 1, half + 2, columns, channels), jnp.bfloat16),
            pltpu.VMEM((9, 3, 2, part, channels), jnp.bfloat16),
            pltpu.VMEM((9, channels, 6 * width), jnp.bfloat16),
            pltpu.VMEM((1, part), jnp.float32),
            pltpu.VMEM((1, width), jnp.float32),
            pltpu.VMEM((frames // 2, half, columns, width), jnp.bfloat16),
            dma, dma, dma((12,)), dma((3,)), dma((3,)), dma, dma,
            dma((BACK,)), dma((BACK,)), dma((BACK,)), dma((BACK,)), dma((BACK,)), dma((BACK,)),
            dma((frames // 2,)), dma((frames // 2,)),
        ],
        compiler_params=pltpu.CompilerParams(
            collective_id=0, has_side_effects=True, vmem_limit_bytes=60000 * 1024
        ),
    )(
        video,
        jnp.swapaxes(first_weight, 3, 4).reshape(9, 3, part, channels),
        first_bias.reshape(1, part),
        second_weight.reshape(9, 3, channels, 2 * width),
        second_bias.reshape(1, width),
    )


def solution(mesh):
    placed = (
        P(("clip", "slab"), "tile", None, None),
        P(None, None, None, None, "chan"),
        P("chan"),
        P(),
        P("chan"),
    )
    return jax.shard_map(
        functools.partial(shards, mesh.shape["tile"], mesh.shape["slab"]),
        mesh=mesh,
        in_specs=placed,
        out_specs=P(("clip", "slab"), "tile", None, "chan"),
        check_vma=False,
    )
```

```python
import functools

import jax
import jax.numpy as jnp
from jax import lax
from jax.experimental import pallas as pl
from jax.experimental.pallas import tpu as pltpu
from jax.sharding import PartitionSpec as P

MESH = pl.DeviceIdType.MESH
BACK = 3


def kernel(
    tiles, slabs, video, w1, b1, w2, b2, out,
    v, h, k1, k2, b1_peer, b2_peer, going,
    local_sem, w1_sem, w2_sem, h_send, h_recv, small_send, small_recv, own_send, own_recv,
    x_send, x_recv, z_send, z_recv, p_send, p_recv, o_send, o_recv,
):
    frames, rows, columns, channels = video.shape
    half = rows // 2
    core = lax.axis_index("chan")
    tile = lax.axis_index("tile")
    slab = lax.axis_index("slab")
    other = 1 - core
    z_tile = tile + 2 * core - 1
    has_z = jnp.logical_and(z_tile >= 0, z_tile < tiles)
    no_z = jnp.logical_or(z_tile < 0, z_tile >= tiles)
    has_next = slab < slabs - 1
    has_prev = slab > 0
    peer = {"chan": other}
    z_peer = {"chan": other, "tile": z_tile}
    following = {"slab": slab + 1}
    preceding = {"slab": slab - 1}

    def remote(src, dst, send, recv, device):
        return pltpu.make_async_remote_copy(
            src_ref=src, dst_ref=dst, send_sem=send, recv_sem=recv,
            device_id=device, device_id_type=MESH,
        )

    mine = pl.ds(half * core, half)
    halo_here = pl.ds(rows * core, half)
    halo_there = pl.ds(rows * other, half)
    inner_here = pl.ds(rows * other, half)
    inner_there = pl.ds(rows * core, half)
    arrived = pl.ds(half, half)

    into_v = pltpu.make_async_copy(
        video.at[pl.ds(0, frames - 1)],
        v.at[pl.ds(BACK, frames - 1), pl.ds(half * other, rows)],
        local_sem,
    )
    into_v.start()
    own_w1 = pltpu.make_async_copy(w1, k1.at[:, :, 0], w1_sem)
    own_w1.start()
    part = channels // 2
    width = b2.shape[1]
    w2_copies = []
    for e in range(3):
        for n in range(2):
            for k in range(2):
                owner_n = core if n == 0 else other
                owner_k = core if k == 0 else other
                w2_copies.append(
                    pltpu.make_async_copy(
                        w2.at[:, e, pl.ds(pl.multiple_of(owner_k * part, part), part),
                              pl.ds(pl.multiple_of(owner_n * width, width), width)],
                        k2.at[:, pl.ds(k * part, part), pl.ds((2 * e + n) * width, width)],
                        w2_sem.at[len(w2_copies)],
                    )
                )
    for copy in w2_copies:
        copy.start()

    barrier = pltpu.get_barrier_semaphore()
    everyone = ((None, peer), (has_z, z_peer), (has_next, following), (has_prev, preceding))

    def when(condition, body):
        if condition is None:
            body()
        else:
            pl.when(condition)(body)

    for condition, device in everyone:
        when(condition, lambda device=device: pl.semaphore_signal(
            barrier, inc=1, device_id=device, device_id_type=MESH))
    met = 1 + sum(jnp.where(condition, 1, 0) for condition, _ in everyone[1:])
    pl.semaphore_wait(barrier, met)

    small = [
        remote(w1, k1.at[:, :, 1], small_send.at[0], small_recv.at[0], peer),
        remote(b1, b1_peer, small_send.at[1], small_recv.at[1], peer),
        remote(b2, b2_peer, small_send.at[2], small_recv.at[2], peer),
    ]
    to_next = [
        remote(video.at[frames - BACK + f, mine], v.at[f, arrived], x_send.at[f], x_recv.at[f], following)
        for f in range(BACK)
    ]
    own_z = remote(
        video.at[pl.ds(0, frames - 1), mine],
        v.at[pl.ds(BACK, frames - 1), halo_there],
        own_send, own_recv, z_peer,
    )
    forward_z = [
        remote(v.at[f, arrived], v.at[f, halo_there], z_send.at[f], z_recv.at[f], z_peer)
        for f in range(BACK)
    ]
    forward_p = [
        remote(v.at[f, arrived], v.at[f, inner_there], p_send.at[f], p_recv.at[f], peer)
        for f in range(BACK)
    ]

    small[0].start()

    @pl.when(has_next)
    def _():
        for f in reversed(range(BACK)):
            to_next[f].start()

    @pl.when(has_z)
    def _():
        own_z.start()

    small[1].start()
    small[2].start()

    @pl.when(no_z)
    def _():
        v[:, halo_here] = jnp.zeros((v.shape[0], half, columns, channels), v.dtype)

    @pl.when(slab == 0)
    def _():
        v[0:BACK] = jnp.zeros((BACK,) + v.shape[1:], v.dtype)
        h[0:2] = jnp.zeros((2,) + h.shape[1:], h.dtype)

    def pass_on(f):
        @pl.when(has_prev)
        def _():
            remote(v.at[f, arrived], v.at[f, arrived], x_send.at[f], x_recv.at[f], preceding).wait_recv()
            forward_p[f].start()

            @pl.when(has_z)
            def _():
                forward_z[f].start()

    def ready(f):
        @pl.when(has_prev)
        def _():
            remote(v.at[f, arrived], v.at[f, inner_here], p_send.at[f], p_recv.at[f], peer).wait_recv()

            @pl.when(has_z)
            def _():
                remote(v.at[f, arrived], v.at[f, halo_here], z_send.at[f], z_recv.at[f], z_peer).wait_recv()

    def taps(source, first, count):
        return jnp.concatenate(
            [
                source[first + a, b : b + count].reshape(count * columns, channels)
                for a in range(3)
                for b in range(3)
            ],
            axis=1,
        )

    def shifted_sum(parts, width, bias):
        size = parts.shape[0]
        column = lax.broadcasted_iota(jnp.int32, (size, width), 0) % columns
        before = pltpu.roll(parts[:, 0:width], 1, 0)
        after = pltpu.roll(parts[:, 2 * width : 3 * width], size - 1, 0)
        total = parts[:, width : 2 * width] + jnp.where(column == 0, 0.0, before)
        total = total + jnp.where(column == columns - 1, 0.0, after) + bias
        return total / (1.0 + jnp.exp(-total))

    def hidden(index):
        count = h.shape[1]
        parts = lax.dot_general(
            taps(v, index - 1, count),
            jnp.concatenate([k1[tap].reshape(3 * channels, channels) for tap in range(9)], axis=1),
            (((1,), (1,)), ((), ())),
            preferred_element_type=jnp.float32,
        )
        bias = jnp.concatenate([b1[...], b1_peer[...]], axis=1)
        value = shifted_sum(parts, channels, bias).astype(h.dtype)
        h[index] = value.reshape(count, columns, channels)

        @pl.when(no_z)
        def _():
            h[index, pl.ds((count - 1) * core, 1)] = jnp.zeros((1, columns, channels), h.dtype)

    to_peer = [
        remote(going.at[t], out.at[t, mine], o_send.at[t], o_recv.at[t], peer)
        for t in range(frames // 2)
    ]

    def latent(t):
        parts = jnp.dot(
            taps(h, 2 * t, half), k2[...].reshape(9 * channels, 6 * width),
            preferred_element_type=jnp.float32,
        )
        bias = jnp.concatenate([b2[...], b2_peer[...]], axis=1)
        value = shifted_sum(parts, 2 * width, bias).astype(out.dtype)
        going[t] = value[:, width:].reshape(half, columns, width)
        to_peer[t].start()
        out[t, mine] = value[:, :width].reshape(half, columns, width)

    small[0].wait_recv()
    own_w1.wait()
    small[1].wait_recv()
    small[2].wait_recv()
    pass_on(2)
    into_v.wait()

    @pl.when(has_z)
    def _():
        remote(
            v.at[pl.ds(BACK, frames - 1), halo_here], v.at[pl.ds(BACK, frames - 1), halo_here],
            own_send, own_recv, z_peer,
        ).wait_recv()

    handed = remote(h.at[frames], h.at[0], h_send, h_recv, following)
    hidden(frames)

    @pl.when(has_next)
    def _():
        handed.start()

    for index in range(4, frames):
        hidden(index)
    pass_on(1)
    ready(2)
    hidden(3)
    pass_on(0)
    ready(1)
    hidden(2)
    for copy in w2_copies:
        copy.wait()
    for t in range(1, frames // 2):
        latent(t)
    ready(0)

    @pl.when(has_prev)
    def _():
        hidden(1)
        remote(h.at[0], h.at[0], h_send, h_recv, preceding).wait_recv()

    latent(0)

    for copy in small:
        copy.wait_send()

    @pl.when(has_next)
    def _():
        for copy in to_next:
            copy.wait_send()
        handed.wait_send()

    @pl.when(has_z)
    def _():
        own_z.wait_send()

    @pl.when(has_prev)
    def _():
        for copy in forward_p:
            copy.wait_send()

        @pl.when(has_z)
        def _():
            for copy in forward_z:
                copy.wait_send()

    theirs = pl.ds(half * other, half)
    for t in range(frames // 2):
        remote(going.at[t], out.at[t, theirs], o_send.at[t], o_recv.at[t], peer).wait_recv()
        to_peer[t].wait_send()


def shards(tiles, slabs, video, first_weight, first_bias, second_weight, second_bias):
    frames, rows, columns, channels = video.shape
    half = rows // 2
    assert half == 2 and frames >= 4 and frames % 2 == 0
    part = first_bias.shape[0]
    width = second_bias.shape[0]
    anywhere = pl.BlockSpec(memory_space=pltpu.HBM)
    inside = pl.BlockSpec(memory_space=pltpu.VMEM)
    dma = pltpu.SemaphoreType.DMA
    return pl.pallas_call(
        functools.partial(kernel, tiles, slabs),
        out_shape=jax.ShapeDtypeStruct((frames // 2, rows, columns, width), jnp.bfloat16),
        in_specs=[anywhere, anywhere, inside, anywhere, inside],
        out_specs=inside,
        scratch_shapes=[
            pltpu.VMEM((BACK + frames - 1, rows + 2, columns, channels), jnp.bfloat16),
            pltpu.VMEM((frames + 1, half + 2, columns, channels), jnp.bfloat16),
            pltpu.VMEM((9, 3, 2, part, channels), jnp.bfloat16),
            pltpu.VMEM((9, channels, 6 * width), jnp.bfloat16),
            pltpu.VMEM((1, part), jnp.float32),
            pltpu.VMEM((1, width), jnp.float32),
            pltpu.VMEM((frames // 2, half, columns, width), jnp.bfloat16),
            dma, dma, dma((12,)), dma, dma, dma((3,)), dma((3,)), dma, dma,
            dma((BACK,)), dma((BACK,)), dma((BACK,)), dma((BACK,)), dma((BACK,)), dma((BACK,)),
            dma((frames // 2,)), dma((frames // 2,)),
        ],
        compiler_params=pltpu.CompilerParams(
            collective_id=0, has_side_effects=True, vmem_limit_bytes=58000 << 10
        ),
    )(
        video,
        jnp.swapaxes(first_weight, 3, 4).reshape(9, 3, part, channels),
        first_bias.reshape(1, part),
        second_weight.reshape(9, 3, channels, 2 * width),
        second_bias.reshape(1, width),
    )


def solution(mesh):
    placed = (
        P(("clip", "slab"), "tile", None, None),
        P(None, None, None, None, "chan"),
        P("chan"),
        P(),
        P("chan"),
    )
    return jax.shard_map(
        functools.partial(shards, mesh.shape["tile"], mesh.shape["slab"]),
        mesh=mesh,
        in_specs=placed,
        out_specs=P(("clip", "slab"), "tile", None, "chan"),
        check_vma=False,
    )
```

```python
import functools

import jax
import jax.numpy as jnp
from jax import lax
from jax.experimental import pallas as pl
from jax.experimental.pallas import tpu as pltpu
from jax.sharding import PartitionSpec as P

MESH = pl.DeviceIdType.MESH
BACK = 3


def kernel(
    tiles, slabs, video, w1, b1, w2, b2, out,
    v, h, k1, k2, b1_peer, b2_peer, going,
    local_sem, w1_sem, w2_sem, h_send, h_recv, small_send, small_recv, own_send, own_recv,
    x_send, x_recv, z_send, z_recv, p_send, p_recv, o_send, o_recv,
):
    frames, rows, columns, channels = video.shape
    half = rows // 2
    core = lax.axis_index("chan")
    tile = lax.axis_index("tile")
    slab = lax.axis_index("slab")
    other = 1 - core
    z_tile = tile + 2 * core - 1
    has_z = jnp.logical_and(z_tile >= 0, z_tile < tiles)
    no_z = jnp.logical_or(z_tile < 0, z_tile >= tiles)
    has_next = slab < slabs - 1
    has_prev = slab > 0
    peer = {"chan": other}
    z_peer = {"chan": other, "tile": z_tile}
    following = {"slab": slab + 1}
    preceding = {"slab": slab - 1}

    def remote(src, dst, send, recv, device):
        return pltpu.make_async_remote_copy(
            src_ref=src, dst_ref=dst, send_sem=send, recv_sem=recv,
            device_id=device, device_id_type=MESH,
        )

    mine = pl.ds(half * core, half)
    halo_here = pl.ds(rows * core, half)
    halo_there = pl.ds(rows * other, half)
    inner_here = pl.ds(rows * other, half)
    inner_there = pl.ds(rows * core, half)
    arrived = pl.ds(half, half)

    into_v = pltpu.make_async_copy(
        video.at[pl.ds(0, frames - 1)],
        v.at[pl.ds(BACK, frames - 1), pl.ds(half * other, rows)],
        local_sem,
    )
    into_v.start()
    own_w1 = pltpu.make_async_copy(w1, k1.at[:, :, 0], w1_sem)
    own_w1.start()
    part = channels // 2
    width = b2.shape[1]
    w2_copies = []
    for e in range(3):
        for n in range(2):
            for k in range(2):
                owner_n = core if n == 0 else other
                owner_k = core if k == 0 else other
                w2_copies.append(
                    pltpu.make_async_copy(
                        w2.at[:, e, pl.ds(pl.multiple_of(owner_k * part, part), part),
                              pl.ds(pl.multiple_of(owner_n * width, width), width)],
                        k2.at[:, pl.ds(k * part, part), pl.ds((2 * e + n) * width, width)],
                        w2_sem.at[len(w2_copies)],
                    )
                )
    for copy in w2_copies:
        copy.start()

    barrier = pltpu.get_barrier_semaphore()
    everyone = ((None, peer), (has_z, z_peer), (has_next, following), (has_prev, preceding))

    def when(condition, body):
        if condition is None:
            body()
        else:
            pl.when(condition)(body)

    for condition, device in everyone:
        when(condition, lambda device=device: pl.semaphore_signal(
            barrier, inc=1, device_id=device, device_id_type=MESH))
    met = 1 + sum(jnp.where(condition, 1, 0) for condition, _ in everyone[1:])
    pl.semaphore_wait(barrier, met)

    small = [
        remote(w1, k1.at[:, :, 1], small_send.at[0], small_recv.at[0], peer),
        remote(b1, b1_peer, small_send.at[1], small_recv.at[1], peer),
        remote(b2, b2_peer, small_send.at[2], small_recv.at[2], peer),
    ]
    to_next = [
        remote(video.at[frames - BACK + f, mine], v.at[f, arrived], x_send.at[f], x_recv.at[f], following)
        for f in range(BACK)
    ]
    own_z = remote(
        video.at[pl.ds(0, frames - 1), mine],
        v.at[pl.ds(BACK, frames - 1), halo_there],
        own_send, own_recv, z_peer,
    )
    forward_z = [
        remote(v.at[f, arrived], v.at[f, halo_there], z_send.at[f], z_recv.at[f], z_peer)
        for f in range(BACK)
    ]
    forward_p = [
        remote(v.at[f, arrived], v.at[f, inner_there], p_send.at[f], p_recv.at[f], peer)
        for f in range(BACK)
    ]

    small[0].start()

    @pl.when(has_next)
    def _():
        for f in reversed(range(BACK)):
            to_next[f].start()

    @pl.when(has_z)
    def _():
        own_z.start()

    small[1].start()
    small[2].start()

    @pl.when(no_z)
    def _():
        v[:, halo_here] = jnp.zeros((v.shape[0], half, columns, channels), v.dtype)

    @pl.when(slab == 0)
    def _():
        v[0:BACK] = jnp.zeros((BACK,) + v.shape[1:], v.dtype)
        h[0:2] = jnp.zeros((2,) + h.shape[1:], h.dtype)

    def pass_on(f):
        @pl.when(has_prev)
        def _():
            remote(v.at[f, arrived], v.at[f, arrived], x_send.at[f], x_recv.at[f], preceding).wait_recv()
            forward_p[f].start()

            @pl.when(has_z)
            def _():
                forward_z[f].start()

    def inner_ready(f):
        @pl.when(has_prev)
        def _():
            remote(v.at[f, arrived], v.at[f, inner_here], p_send.at[f], p_recv.at[f], peer).wait_recv()

    def outer_ready(f):
        @pl.when(jnp.logical_and(has_prev, has_z))
        def _():
            remote(v.at[f, arrived], v.at[f, halo_here], z_send.at[f], z_recv.at[f], z_peer).wait_recv()

    def taps(source, index, first, count):
        return jnp.concatenate(
            [
                source[index + a, pl.ds(first + b, count)].reshape(count * columns, channels)
                for a in range(3)
                for b in range(3)
            ],
            axis=1,
        )

    def shifted_sum(parts, width, bias):
        size = parts.shape[0]
        column = lax.broadcasted_iota(jnp.int32, (size, width), 0) % columns
        before = pltpu.roll(parts[:, 0:width], 1, 0)
        after = pltpu.roll(parts[:, 2 * width : 3 * width], size - 1, 0)
        total = parts[:, width : 2 * width] + jnp.where(column == 0, 0.0, before)
        total = total + jnp.where(column == columns - 1, 0.0, after) + bias
        return total / (1.0 + jnp.exp(-total))

    def hidden_rows(index, first):
        parts = lax.dot_general(
            taps(v, index - 1, first, half),
            jnp.concatenate([k1[tap].reshape(3 * channels, channels) for tap in range(9)], axis=1),
            (((1,), (1,)), ((), ())),
            preferred_element_type=jnp.float32,
        )
        bias = jnp.concatenate([b1[...], b1_peer[...]], axis=1)
        value = shifted_sum(parts, channels, bias).astype(h.dtype)
        h[index, pl.ds(first, half)] = value.reshape(half, columns, channels)

    def inner(index):
        hidden_rows(index, half * other)

    def outer(index):
        hidden_rows(index, half * core)

        @pl.when(no_z)
        def _():
            h[index, pl.ds((rows - 1) * core, 1)] = jnp.zeros((1, columns, channels), h.dtype)

    to_peer = [
        remote(going.at[t], out.at[t, mine], o_send.at[t], o_recv.at[t], peer)
        for t in range(frames // 2)
    ]

    def latent(t):
        parts = jnp.dot(
            taps(h, 2 * t, 0, half), k2[...].reshape(9 * channels, 6 * width),
            preferred_element_type=jnp.float32,
        )
        bias = jnp.concatenate([b2[...], b2_peer[...]], axis=1)
        value = shifted_sum(parts, 2 * width, bias).astype(out.dtype)
        going[t] = value[:, width:].reshape(half, columns, width)
        to_peer[t].start()
        out[t, mine] = value[:, :width].reshape(half, columns, width)

    small[0].wait_recv()
    own_w1.wait()
    small[1].wait_recv()
    small[2].wait_recv()
    into_v.wait()
    handed = remote(h.at[frames], h.at[0], h_send, h_recv, following)
    inner(frames)
    pass_on(2)

    @pl.when(has_z)
    def _():
        remote(
            v.at[pl.ds(BACK, frames - 1), halo_here], v.at[pl.ds(BACK, frames - 1), halo_here],
            own_send, own_recv, z_peer,
        ).wait_recv()

    outer(frames)

    @pl.when(has_next)
    def _():
        handed.start()

    pass_on(1)
    inner_ready(2)
    for index in range(frames - 1, 3, -1):
        inner(index)
        outer(index)
    inner(3)
    pass_on(0)
    outer_ready(2)
    outer(3)
    inner_ready(1)
    inner(2)
    outer_ready(1)
    outer(2)
    for copy in w2_copies:
        copy.wait()
    for t in range(1, frames // 2):
        latent(t)
    inner_ready(0)

    @pl.when(has_prev)
    def _():
        inner(1)
        outer_ready(0)
        outer(1)
        remote(h.at[0], h.at[0], h_send, h_recv, preceding).wait_recv()

    latent(0)

    for copy in small:
        copy.wait_send()

    @pl.when(has_next)
    def _():
        for copy in to_next:
            copy.wait_send()
        handed.wait_send()

    @pl.when(has_z)
    def _():
        own_z.wait_send()

    @pl.when(has_prev)
    def _():
        for copy in forward_p:
            copy.wait_send()

        @pl.when(has_z)
        def _():
            for copy in forward_z:
                copy.wait_send()

    theirs = pl.ds(half * other, half)
    for t in range(frames // 2):
        remote(going.at[t], out.at[t, theirs], o_send.at[t], o_recv.at[t], peer).wait_recv()
        to_peer[t].wait_send()


def shards(tiles, slabs, video, first_weight, first_bias, second_weight, second_bias):
    frames, rows, columns, channels = video.shape
    half = rows // 2
    assert half == 2 and frames >= 4 and frames % 2 == 0
    part = first_bias.shape[0]
    width = second_bias.shape[0]
    anywhere = pl.BlockSpec(memory_space=pltpu.HBM)
    inside = pl.BlockSpec(memory_space=pltpu.VMEM)
    dma = pltpu.SemaphoreType.DMA
    return pl.pallas_call(
        functools.partial(kernel, tiles, slabs),
        out_shape=jax.ShapeDtypeStruct((frames // 2, rows, columns, width), jnp.bfloat16),
        in_specs=[anywhere, anywhere, inside, anywhere, inside],
        out_specs=inside,
        scratch_shapes=[
            pltpu.VMEM((BACK + frames - 1, rows + 2, columns, channels), jnp.bfloat16),
            pltpu.VMEM((frames + 1, half + 2, columns, channels), jnp.bfloat16),
            pltpu.VMEM((9, 3, 2, part, channels), jnp.bfloat16),
            pltpu.VMEM((9, channels, 6 * width), jnp.bfloat16),
            pltpu.VMEM((1, part), jnp.float32),
            pltpu.VMEM((1, width), jnp.float32),
            pltpu.VMEM((frames // 2, half, columns, width), jnp.bfloat16),
            dma, dma, dma((12,)), dma, dma, dma((3,)), dma((3,)), dma, dma,
            dma((BACK,)), dma((BACK,)), dma((BACK,)), dma((BACK,)), dma((BACK,)), dma((BACK,)),
            dma((frames // 2,)), dma((frames // 2,)),
        ],
        compiler_params=pltpu.CompilerParams(
            collective_id=0, has_side_effects=True, vmem_limit_bytes=32 << 20
        ),
    )(
        *(
            pltpu.with_memory_space_constraint(operand, pltpu.HBM)
            for operand in (
                video,
                jnp.swapaxes(first_weight, 3, 4).reshape(9, 3, part, channels),
                first_bias.reshape(1, part),
                second_weight.reshape(9, 3, channels, 2 * width),
                second_bias.reshape(1, width),
            )
        )
    )


def solution(mesh):
    placed = (
        P(("clip", "slab"), "tile", None, None),
        P(None, None, None, None, "chan"),
        P("chan"),
        P(),
        P("chan"),
    )
    return jax.shard_map(
        functools.partial(shards, mesh.shape["tile"], mesh.shape["slab"]),
        mesh=mesh,
        in_specs=placed,
        out_specs=P(("clip", "slab"), "tile", None, "chan"),
        check_vma=False,
    )
```

```python
import functools

import jax
import jax.numpy as jnp
from jax import lax
from jax.experimental import pallas as pl
from jax.experimental.pallas import tpu as pltpu
from jax.sharding import PartitionSpec as P

MESH = pl.DeviceIdType.MESH
BACK = 3


def kernel(
    tiles, slabs, video, w1, b1, w2, b2, out,
    v, h, k1, k2, b1_peer, b2_peer, going,
    local_sem, w1_sem, w2_sem, h_send, h_recv, small_send, small_recv, own_send, own_recv,
    x_send, x_recv, z_send, z_recv, p_send, p_recv, o_send, o_recv,
):
    frames, rows, columns, channels = video.shape
    half = rows // 2
    core = lax.axis_index("chan")
    tile = lax.axis_index("tile")
    slab = lax.axis_index("slab")
    other = 1 - core
    z_tile = tile + 2 * core - 1
    has_z = jnp.logical_and(z_tile >= 0, z_tile < tiles)
    no_z = jnp.logical_or(z_tile < 0, z_tile >= tiles)
    has_next = slab < slabs - 1
    has_prev = slab > 0
    peer = {"chan": other}
    z_peer = {"chan": other, "tile": z_tile}
    following = {"slab": slab + 1}
    preceding = {"slab": slab - 1}

    def remote(src, dst, send, recv, device):
        return pltpu.make_async_remote_copy(
            src_ref=src, dst_ref=dst, send_sem=send, recv_sem=recv,
            device_id=device, device_id_type=MESH,
        )

    mine = pl.ds(half * core, half)
    halo_here = pl.ds(rows * core, half)
    halo_there = pl.ds(rows * other, half)
    inner_here = pl.ds(rows * other, half)
    inner_there = pl.ds(rows * core, half)
    arrived = pl.ds(half, half)

    into_v = pltpu.make_async_copy(
        video,
        v.at[pl.ds(BACK, frames), pl.ds(half * other, rows)],
        local_sem,
    )
    into_v.start()
    own_w1 = pltpu.make_async_copy(w1, k1.at[:, :, 0], w1_sem)
    own_w1.start()
    part = channels // 2
    width = b2.shape[1]
    w2_copies = []
    for e in range(3):
        for n in range(2):
            for k in range(2):
                owner_n = core if n == 0 else other
                owner_k = core if k == 0 else other
                w2_copies.append(
                    pltpu.make_async_copy(
                        w2.at[:, e, pl.ds(pl.multiple_of(owner_k * part, part), part),
                              pl.ds(pl.multiple_of(owner_n * width, width), width)],
                        k2.at[:, pl.ds(k * part, part), pl.ds((2 * e + n) * width, width)],
                        w2_sem.at[len(w2_copies)],
                    )
                )
    barrier = pltpu.get_barrier_semaphore()
    everyone = ((None, peer), (has_z, z_peer), (has_next, following), (has_prev, preceding))

    def when(condition, body):
        if condition is None:
            body()
        else:
            pl.when(condition)(body)

    for condition, device in everyone:
        when(condition, lambda device=device: pl.semaphore_signal(
            barrier, inc=1, device_id=device, device_id_type=MESH))
    into_v.wait()
    own_w1.wait()
    met = 1 + sum(jnp.where(condition, 1, 0) for condition, _ in everyone[1:])
    pl.semaphore_wait(barrier, met)

    small = [
        remote(k1.at[:, :, 0], k1.at[:, :, 1], small_send.at[0], small_recv.at[0], peer),
        remote(b1, b1_peer, small_send.at[1], small_recv.at[1], peer),
        remote(b2, b2_peer, small_send.at[2], small_recv.at[2], peer),
    ]
    to_next = [
        remote(v.at[frames + f, arrived], v.at[f, arrived], x_send.at[f], x_recv.at[f], following)
        for f in range(BACK)
    ]
    own_z = remote(
        v.at[pl.ds(BACK, frames - 1), arrived],
        v.at[pl.ds(BACK, frames - 1), halo_there],
        own_send, own_recv, z_peer,
    )
    forward_z = [
        remote(v.at[f, arrived], v.at[f, halo_there], z_send.at[f], z_recv.at[f], z_peer)
        for f in range(BACK)
    ]
    forward_p = [
        remote(v.at[f, arrived], v.at[f, inner_there], p_send.at[f], p_recv.at[f], peer)
        for f in range(BACK)
    ]

    small[0].start()

    @pl.when(has_next)
    def _():
        for f in reversed(range(BACK)):
            to_next[f].start()

    @pl.when(has_z)
    def _():
        own_z.start()

    small[1].start()
    small[2].start()
    for copy in w2_copies:
        copy.start()

    @pl.when(no_z)
    def _():
        v[:, halo_here] = jnp.zeros((v.shape[0], half, columns, channels), v.dtype)

    @pl.when(slab == 0)
    def _():
        v[0:BACK] = jnp.zeros((BACK,) + v.shape[1:], v.dtype)
        h[0:2] = jnp.zeros((2,) + h.shape[1:], h.dtype)

    def pass_on(f):
        @pl.when(has_prev)
        def _():
            remote(v.at[f, arrived], v.at[f, arrived], x_send.at[f], x_recv.at[f], preceding).wait_recv()
            forward_p[f].start()

            @pl.when(has_z)
            def _():
                forward_z[f].start()

    def inner_ready(f):
        @pl.when(has_prev)
        def _():
            remote(v.at[f, arrived], v.at[f, inner_here], p_send.at[f], p_recv.at[f], peer).wait_recv()

    def outer_ready(f):
        @pl.when(jnp.logical_and(has_prev, has_z))
        def _():
            remote(v.at[f, arrived], v.at[f, halo_here], z_send.at[f], z_recv.at[f], z_peer).wait_recv()

    def taps(source, index, first, count):
        return jnp.concatenate(
            [
                source[index + a, pl.ds(first + b, count)].reshape(count * columns, channels)
                for a in range(3)
                for b in range(3)
            ],
            axis=1,
        )

    def shifted_sum(parts, width, bias):
        size = parts.shape[0]
        column = lax.broadcasted_iota(jnp.int32, (size, width), 0) % columns
        before = pltpu.roll(parts[:, 0:width], 1, 0)
        after = pltpu.roll(parts[:, 2 * width : 3 * width], size - 1, 0)
        total = parts[:, width : 2 * width] + jnp.where(column == 0, 0.0, before)
        total = total + jnp.where(column == columns - 1, 0.0, after) + bias
        return total / (1.0 + jnp.exp(-total))

    def hidden_rows(index, first, count):
        parts = lax.dot_general(
            taps(v, index - 1, first, count),
            jnp.concatenate([k1[tap].reshape(3 * channels, channels) for tap in range(9)], axis=1),
            (((1,), (1,)), ((), ())),
            preferred_element_type=jnp.float32,
        )
        bias = jnp.concatenate([b1[...], b1_peer[...]], axis=1)
        value = shifted_sum(parts, channels, bias).astype(h.dtype)
        h[index, pl.ds(first, count)] = value.reshape(count, columns, channels)

    def inner(index):
        hidden_rows(index, half * other, half)

    def outer(index):
        hidden_rows(index, half * core, half)
        clear_outside(index)

    def whole(index):
        hidden_rows(index, 0, rows)
        clear_outside(index)

    def clear_outside(index):
        @pl.when(no_z)
        def _():
            h[index, pl.ds((rows - 1) * core, 1)] = jnp.zeros((1, columns, channels), h.dtype)

    to_peer = [
        remote(going.at[t], out.at[t, mine], o_send.at[t], o_recv.at[t], peer)
        for t in range(frames // 2)
    ]

    def latent(t):
        parts = jnp.dot(
            taps(h, 2 * t, 0, half), k2[...].reshape(9 * channels, 6 * width),
            preferred_element_type=jnp.float32,
        )
        for start, bias in ((width, b2_peer[...]), (0, b2[...])):
            chosen = jnp.concatenate(
                [
                    parts[:, 2 * width * e + start : 2 * width * e + start + width]
                    for e in range(3)
                ],
                axis=1,
            )
            value = shifted_sum(chosen, width, bias).astype(out.dtype).reshape(half, columns, width)
            if start:
                going[t] = value
                to_peer[t].start()
            else:
                out[t, mine] = value

    small[0].wait_recv()
    small[1].wait_recv()
    small[2].wait_recv()
    handed = remote(h.at[frames], h.at[0], h_send, h_recv, following)
    inner(frames)
    pass_on(2)

    @pl.when(has_z)
    def _():
        remote(
            v.at[pl.ds(BACK, frames - 1), halo_here], v.at[pl.ds(BACK, frames - 1), halo_here],
            own_send, own_recv, z_peer,
        ).wait_recv()

    outer(frames)

    @pl.when(has_next)
    def _():
        handed.start()

    pass_on(1)
    inner_ready(2)
    for index in range(frames - 1, 3, -1):
        inner(index)
        outer(index)
    inner(3)
    pass_on(0)
    outer_ready(2)
    outer(3)
    inner_ready(1)
    inner(2)
    outer_ready(1)
    outer(2)
    for copy in w2_copies:
        copy.wait()
    for t in range(1, frames // 2):
        latent(t)
    inner_ready(0)

    @pl.when(has_prev)
    def _():
        outer_ready(0)
        whole(1)
        remote(h.at[0], h.at[0], h_send, h_recv, preceding).wait_recv()

    latent(0)

    for copy in small:
        copy.wait_send()

    @pl.when(has_next)
    def _():
        for copy in to_next:
            copy.wait_send()
        handed.wait_send()

    @pl.when(has_z)
    def _():
        own_z.wait_send()

    @pl.when(has_prev)
    def _():
        for copy in forward_p:
            copy.wait_send()

        @pl.when(has_z)
        def _():
            for copy in forward_z:
                copy.wait_send()

    theirs = pl.ds(half * other, half)
    for t in range(frames // 2):
        remote(going.at[t], out.at[t, theirs], o_send.at[t], o_recv.at[t], peer).wait_recv()
        to_peer[t].wait_send()


def shards(tiles, slabs, video, first_weight, first_bias, second_weight, second_bias):
    frames, rows, columns, channels = video.shape
    half = rows // 2
    assert half == 2 and frames >= 4 and frames % 2 == 0
    part = first_bias.shape[0]
    width = second_bias.shape[0]
    anywhere = pl.BlockSpec(memory_space=pltpu.HBM)
    inside = pl.BlockSpec(memory_space=pltpu.VMEM)
    dma = pltpu.SemaphoreType.DMA
    return pl.pallas_call(
        functools.partial(kernel, tiles, slabs),
        out_shape=jax.ShapeDtypeStruct((frames // 2, rows, columns, width), jnp.bfloat16),
        in_specs=[anywhere, anywhere, inside, anywhere, inside],
        out_specs=inside,
        scratch_shapes=[
            pltpu.VMEM((BACK + frames, rows + 2, columns, channels), jnp.bfloat16),
            pltpu.VMEM((frames + 1, half + 2, columns, channels), jnp.bfloat16),
            pltpu.VMEM((9, 3, 2, part, channels), jnp.bfloat16),
            pltpu.VMEM((9, channels, 6 * width), jnp.bfloat16),
            pltpu.VMEM((1, part), jnp.float32),
            pltpu.VMEM((1, width), jnp.float32),
            pltpu.VMEM((frames // 2, half, columns, width), jnp.bfloat16),
            dma, dma, dma((12,)), dma, dma, dma((3,)), dma((3,)), dma, dma,
            dma((BACK,)), dma((BACK,)), dma((BACK,)), dma((BACK,)), dma((BACK,)), dma((BACK,)),
            dma((frames // 2,)), dma((frames // 2,)),
        ],
        compiler_params=pltpu.CompilerParams(
            collective_id=0, has_side_effects=True, vmem_limit_bytes=32 << 20
        ),
    )(
        *(
            pltpu.with_memory_space_constraint(operand, pltpu.HBM)
            for operand in (
                video,
                jnp.swapaxes(first_weight, 3, 4).reshape(9, 3, part, channels),
                first_bias.reshape(1, part),
                second_weight.reshape(9, 3, channels, 2 * width),
                second_bias.reshape(1, width),
            )
        )
    )


def solution(mesh):
    placed = (
        P(("clip", "slab"), "tile", None, None),
        P(None, None, None, None, "chan"),
        P("chan"),
        P(),
        P("chan"),
    )
    return jax.shard_map(
        functools.partial(shards, mesh.shape["tile"], mesh.shape["slab"]),
        mesh=mesh,
        in_specs=placed,
        out_specs=P(("clip", "slab"), "tile", None, "chan"),
        check_vma=False,
    )
```

```python
import functools

import jax
import jax.numpy as jnp
from jax import lax
from jax.experimental import pallas as pl
from jax.experimental.pallas import tpu as pltpu
from jax.sharding import PartitionSpec as P

MESH = pl.DeviceIdType.MESH
BACK = 2


def kernel(
    tiles, slabs, video, w1, b1, w2, b2, out,
    v, h, k1, k2, b1_peer, b2_peer, going,
    local_sem, w1_sem, w2_sem, h_send, h_recv, e_send, e_recv, q_send, q_recv, small_send, small_recv, own_send, own_recv,
    x_send, x_recv, z_send, z_recv, p_send, p_recv, o_send, o_recv,
):
    frames, rows, columns, channels = video.shape
    half = rows // 2
    core = lax.axis_index("chan")
    tile = lax.axis_index("tile")
    slab = lax.axis_index("slab")
    other = 1 - core
    z_tile = tile + 2 * core - 1
    has_z = jnp.logical_and(z_tile >= 0, z_tile < tiles)
    no_z = jnp.logical_or(z_tile < 0, z_tile >= tiles)
    has_next = slab < slabs - 1
    has_prev = slab > 0
    peer = {"chan": other}
    z_peer = {"chan": other, "tile": z_tile}
    following = {"slab": slab + 1}
    preceding = {"slab": slab - 1}

    def remote(src, dst, send, recv, device):
        return pltpu.make_async_remote_copy(
            src_ref=src, dst_ref=dst, send_sem=send, recv_sem=recv,
            device_id=device, device_id_type=MESH,
        )

    mine = pl.ds(half * core, half)
    halo_here = pl.ds(rows * core, half)
    halo_there = pl.ds(rows * other, half)
    inner_here = pl.ds(rows * other, half)
    inner_there = pl.ds(rows * core, half)
    arrived = pl.ds(half, half)

    into_v = pltpu.make_async_copy(
        video,
        v.at[pl.ds(BACK, frames), pl.ds(half * other, rows)],
        local_sem,
    )
    into_v.start()
    own_w1 = pltpu.make_async_copy(w1, k1.at[:, :, 0], w1_sem)
    own_w1.start()
    part = channels // 2
    width = b2.shape[1]
    w2_copies = []
    for e in range(3):
        for n in range(2):
            for k in range(2):
                owner_n = core if n == 0 else other
                owner_k = core if k == 0 else other
                w2_copies.append(
                    pltpu.make_async_copy(
                        w2.at[:, e, pl.ds(pl.multiple_of(owner_k * part, part), part),
                              pl.ds(pl.multiple_of(owner_n * width, width), width)],
                        k2.at[:, pl.ds(k * part, part), pl.ds((2 * e + n) * width, width)],
                        w2_sem.at[len(w2_copies)],
                    )
                )
    barrier = pltpu.get_barrier_semaphore()
    everyone = ((None, peer), (has_z, z_peer), (has_next, following), (has_prev, preceding))

    def when(condition, body):
        if condition is None:
            body()
        else:
            pl.when(condition)(body)

    for condition, device in everyone:
        when(condition, lambda device=device: pl.semaphore_signal(
            barrier, inc=1, device_id=device, device_id_type=MESH))
    into_v.wait()
    own_w1.wait()
    met = 1 + sum(jnp.where(condition, 1, 0) for condition, _ in everyone[1:])
    pl.semaphore_wait(barrier, met)

    small = [
        remote(k1.at[:, :, 0], k1.at[:, :, 1], small_send.at[0], small_recv.at[0], peer),
        remote(b1, b1_peer, small_send.at[1], small_recv.at[1], peer),
        remote(b2, b2_peer, small_send.at[2], small_recv.at[2], peer),
    ]
    to_next = [
        remote(v.at[frames + f, arrived], v.at[f, arrived], x_send.at[f], x_recv.at[f], following)
        for f in range(BACK)
    ]
    own_z = remote(
        v.at[pl.ds(BACK, frames), arrived],
        v.at[pl.ds(BACK, frames), halo_there],
        own_send, own_recv, z_peer,
    )
    forward_z = [
        remote(v.at[f, arrived], v.at[f, halo_there], z_send.at[f], z_recv.at[f], z_peer)
        for f in range(BACK)
    ]
    forward_p = [
        remote(v.at[f, arrived], v.at[f, inner_there], p_send.at[f], p_recv.at[f], peer)
        for f in range(BACK)
    ]

    small[0].start()

    @pl.when(has_next)
    def _():
        for f in reversed(range(BACK)):
            to_next[f].start()

    @pl.when(has_z)
    def _():
        own_z.start()

    small[1].start()
    small[2].start()
    for copy in w2_copies:
        copy.start()

    @pl.when(no_z)
    def _():
        v[:, halo_here] = jnp.zeros((v.shape[0], half, columns, channels), v.dtype)

    def pass_on(f):
        @pl.when(has_prev)
        def _():
            remote(v.at[f, arrived], v.at[f, arrived], x_send.at[f], x_recv.at[f], preceding).wait_recv()
            forward_p[f].start()

            @pl.when(has_z)
            def _():
                forward_z[f].start()

    def inner_ready(f):
        @pl.when(has_prev)
        def _():
            remote(v.at[f, arrived], v.at[f, inner_here], p_send.at[f], p_recv.at[f], peer).wait_recv()

    def outer_ready(f):
        @pl.when(jnp.logical_and(has_prev, has_z))
        def _():
            remote(v.at[f, arrived], v.at[f, halo_here], z_send.at[f], z_recv.at[f], z_peer).wait_recv()

    def taps(source, index, first, count, oldest=0):
        return jnp.concatenate(
            [
                source[index + a, pl.ds(first + b, count)].reshape(count * columns, channels)
                for a in range(oldest, 3)
                for b in range(3)
            ],
            axis=1,
        )

    def shifted_sum(parts, width, bias):
        size = parts.shape[0]
        column = lax.broadcasted_iota(jnp.int32, (size, width), 0) % columns
        before = pltpu.roll(parts[:, 0:width], 1, 0)
        after = pltpu.roll(parts[:, 2 * width : 3 * width], size - 1, 0)
        total = parts[:, width : 2 * width] + jnp.where(column == 0, 0.0, before)
        total = total + jnp.where(column == columns - 1, 0.0, after) + bias
        return total / (1.0 + jnp.exp(-total))

    def hidden_rows(index, first, count, oldest=0):
        parts = lax.dot_general(
            taps(v, index - 2, first, count, oldest),
            jnp.concatenate([k1[tap].reshape(3 * channels, channels) for tap in range(3 * oldest, 9)], axis=1),
            (((1,), (1,)), ((), ())),
            preferred_element_type=jnp.float32,
        )
        bias = jnp.concatenate([b1[...], b1_peer[...]], axis=1)
        value = shifted_sum(parts, channels, bias).astype(h.dtype)
        h[index, pl.ds(first, count)] = value.reshape(count, columns, channels)

    def inner(index):
        hidden_rows(index, half * other, half)

    def outer(index):
        hidden_rows(index, half * core, half)
        clear_outside(index)

    def whole(index, oldest=0):
        hidden_rows(index, 0, rows, oldest)
        clear_outside(index)

    def clear_outside(index):
        @pl.when(no_z)
        def _():
            h[index, pl.ds((rows - 1) * core, 1)] = jnp.zeros((1, columns, channels), h.dtype)

    to_peer = [
        remote(going.at[t], out.at[t, mine], o_send.at[t], o_recv.at[t], peer)
        for t in range(frames // 2)
    ]

    def latent(t, oldest=0):
        parts = jnp.dot(
            taps(h, 2 * t, 0, half, oldest),
            k2[3 * oldest :].reshape((9 - 3 * oldest) * channels, 6 * width),
            preferred_element_type=jnp.float32,
        )
        for start, bias in ((width, b2_peer[...]), (0, b2[...])):
            chosen = jnp.concatenate(
                [
                    parts[:, 2 * width * e + start : 2 * width * e + start + width]
                    for e in range(3)
                ],
                axis=1,
            )
            value = shifted_sum(chosen, width, bias).astype(out.dtype).reshape(half, columns, width)
            if start:
                going[t] = value
                to_peer[t].start()
            else:
                out[t, mine] = value

    small[0].wait_recv()
    small[1].wait_recv()
    small[2].wait_recv()
    early = pl.ds(2 - core, 1)
    early_there = pl.ds((rows - 1) * core, 1)
    early_here = pl.ds((rows - 1) * other, 1)
    late = pl.ds(half * core, half)
    hand_early = [
        remote(h.at[frames + f, early], h.at[f, early], e_send.at[f], e_recv.at[f], following)
        for f in range(2)
    ]
    hand_late = [
        remote(h.at[frames + f, late], h.at[f, late], h_send.at[f], h_recv.at[f], following)
        for f in range(2)
    ]
    share = [
        remote(h.at[f, early], h.at[f, early_there], q_send.at[f], q_recv.at[f], peer)
        for f in range(2)
    ]

    inner(frames)

    @pl.when(has_next)
    def _():
        hand_early[0].start()
        inner(frames + 1)
        hand_early[1].start()

    pass_on(1)

    @pl.when(has_z)
    def _():
        remote(
            v.at[pl.ds(BACK, frames), halo_here], v.at[pl.ds(BACK, frames), halo_here],
            own_send, own_recv, z_peer,
        ).wait_recv()

    outer(frames)

    @pl.when(has_next)
    def _():
        hand_late[0].start()
        outer(frames + 1)
        hand_late[1].start()

    pass_on(0)
    for index in range(frames - 1, 3, -1):
        whole(index)

    @pl.when(has_prev)
    def _():
        inner_ready(1)
        inner(3)
        outer_ready(1)
        outer(3)
        for f in range(2):
            remote(h.at[f, early], h.at[f, early], e_send.at[f], e_recv.at[f], preceding).wait_recv()
            share[f].start()
        inner_ready(0)
        inner(2)
        outer_ready(0)
        outer(2)

    @pl.when(slab == 0)
    def _():
        whole(3, 1)
        whole(2, 2)

    for copy in w2_copies:
        copy.wait()
    for t in range(1, frames // 2):
        latent(t)

    @pl.when(has_prev)
    def _():
        for f in range(2):
            remote(h.at[f, early], h.at[f, early_here], q_send.at[f], q_recv.at[f], peer).wait_recv()
            remote(h.at[f, late], h.at[f, late], h_send.at[f], h_recv.at[f], preceding).wait_recv()
            shared = h[f, early_here].reshape(columns, channels)
            shared = jnp.concatenate([shared[:, part:], shared[:, :part]], axis=1)
            h[f, early_here] = shared.reshape(1, columns, channels)
        latent(0)

    @pl.when(slab == 0)
    def _():
        latent(0, 2)

    for copy in small:
        copy.wait_send()

    @pl.when(has_next)
    def _():
        for copy in to_next:
            copy.wait_send()
        for copy in hand_early + hand_late:
            copy.wait_send()

    @pl.when(has_z)
    def _():
        own_z.wait_send()

    @pl.when(has_prev)
    def _():
        for copy in forward_p + share:
            copy.wait_send()

        @pl.when(has_z)
        def _():
            for copy in forward_z:
                copy.wait_send()

    theirs = pl.ds(half * other, half)
    for t in range(frames // 2):
        remote(going.at[t], out.at[t, theirs], o_send.at[t], o_recv.at[t], peer).wait_recv()
        to_peer[t].wait_send()


def shards(tiles, slabs, video, first_weight, first_bias, second_weight, second_bias):
    frames, rows, columns, channels = video.shape
    half = rows // 2
    assert half == 2 and frames >= 4 and frames % 2 == 0
    part = first_bias.shape[0]
    width = second_bias.shape[0]
    anywhere = pl.BlockSpec(memory_space=pltpu.HBM)
    inside = pl.BlockSpec(memory_space=pltpu.VMEM)
    dma = pltpu.SemaphoreType.DMA
    return pl.pallas_call(
        functools.partial(kernel, tiles, slabs),
        out_shape=jax.ShapeDtypeStruct((frames // 2, rows, columns, width), jnp.bfloat16),
        in_specs=[anywhere, anywhere, inside, anywhere, inside],
        out_specs=inside,
        scratch_shapes=[
            pltpu.VMEM((BACK + frames, rows + 2, columns, channels), jnp.bfloat16),
            pltpu.VMEM((frames + 2, half + 2, columns, channels), jnp.bfloat16),
            pltpu.VMEM((9, 3, 2, part, channels), jnp.bfloat16),
            pltpu.VMEM((9, channels, 6 * width), jnp.bfloat16),
            pltpu.VMEM((1, part), jnp.float32),
            pltpu.VMEM((1, width), jnp.float32),
            pltpu.VMEM((frames // 2, half, columns, width), jnp.bfloat16),
            dma, dma, dma((12,)), dma((2,)), dma((2,)), dma((2,)), dma((2,)), dma((2,)), dma((2,)), dma((3,)), dma((3,)), dma, dma,
            dma((BACK,)), dma((BACK,)), dma((BACK,)), dma((BACK,)), dma((BACK,)), dma((BACK,)),
            dma((frames // 2,)), dma((frames // 2,)),
        ],
        compiler_params=pltpu.CompilerParams(
            collective_id=0, has_side_effects=True, vmem_limit_bytes=32 << 20
        ),
    )(
        *(
            pltpu.with_memory_space_constraint(operand, pltpu.HBM)
            for operand in (
                video,
                jnp.swapaxes(first_weight, 3, 4).reshape(9, 3, part, channels),
                first_bias.reshape(1, part),
                second_weight.reshape(9, 3, channels, 2 * width),
                second_bias.reshape(1, width),
            )
        )
    )


def solution(mesh):
    placed = (
        P(("clip", "slab"), "tile", None, None),
        P(None, None, None, None, "chan"),
        P("chan"),
        P(),
        P("chan"),
    )
    return jax.shard_map(
        functools.partial(shards, mesh.shape["tile"], mesh.shape["slab"]),
        mesh=mesh,
        in_specs=placed,
        out_specs=P(("clip", "slab"), "tile", None, "chan"),
        check_vma=False,
    )
```
